256 devices in a mesh: circ: 64 (over z, y_hi, x), ax: 4 (over y_lo, core).
Axes of the slice: x: 4, y: 4 (y_hi: 2, y_lo: 2; y = y_hi * 2 + y_lo), z: 8, core: 2. Of those that a mesh axis runs over, the one named last changes fastest.
Arguments:
- fields: float32 [3, 8, 512, 1024], P(None, None, 'circ', 'ax'), may hold values from -6 to 6
Outputs:
- deriv_circ: float32 [3, 8, 512, 1024], P(None, None, 'circ', 'ax')
- deriv_axial: float32 [3, 8, 512, 1024], P(None, None, 'circ', 'ax')
- filtered: float32 [3, 8, 512, 1024], P(None, None, 'circ', 'ax')
The draws below stay inside these ranges and needn't reach their ends.
All inputs are finite; a program needn't handle non-finite values.
Results may differ from the reference program's by a relative error of at most 0.0003.
Values sent between devices are 32-bit elements; how exact they have to be, the bound alone decides.
No kernel may reach another device: no remote copies, remote signals or barrier semaphores. Data moves between devices by JAX's collectives and lax.ppermute only.
A program may use at most 64 MiB of HBM per device.

```python
import jax
import jax.numpy as jnp
from jax import lax

NR = 8
NC = 512
NA = 1024


def levels(rng, dims, pieces, smallest, top_value):
    gain = 1.0
    for axis_at, parts in pieces:
        steps = jax.random.uniform(jax.random.fold_in(jax.random.fold_in(rng, 6), axis_at), (parts,), jnp.float32, smallest / len(pieces), top_value / len(pieces))
        gain = gain * jnp.repeat(jnp.exp(steps), dims[axis_at] // parts).reshape((-1,) + (1,) * (len(dims) - 1 - axis_at))
    return gain


def normal_values(key, extent, width, bound, cuts=(), kind=jnp.bfloat16):
    level = levels(key, extent, cuts, -0.22, 0.18) if cuts else 1.0
    values = jax.random.normal(key, extent, jnp.float32) * width * level
    return jnp.minimum(jnp.maximum(values, -bound), bound).astype(kind)


def setup_inputs(seed: int = 0) -> dict:
    keys = jax.random.split(jax.random.key(seed), 2)
    return {
        "fields": normal_values(keys[0], (3, NR, NC, NA), 1.0, 6.0, ((2, 64), (3, 4)), jnp.float32),
    }


DERIV_NEAR = 14.0 / 9.0
DERIV_FAR = 1.0 / 9.0
ALPHA_DERIV = 1.0 / 3.0
ALPHA_FILTER = 0.4999

def filter_terms(coupling):
    return [(193.0 + 126.0 * coupling) / 256.0, (105.0 + 302.0 * coupling) / 256.0, 15.0 * (2.0 * coupling - 1.0) / 64.0, 45.0 * (1.0 - 2.0 * coupling) / 512.0, 5.0 * (2.0 * coupling - 1.0) / 256.0, (1.0 - 2.0 * coupling) / 512.0]

def periodic_solve(right_side, coupling):
    length = right_side.shape[2]
    mode_index = jnp.arange(length).astype(right_side.dtype)
    eigenvalues = 1.0 + 2.0 * coupling * jnp.cos(2.0 * jnp.pi * mode_index / length)
    spectrum = jnp.fft.fft(right_side, axis=2) / eigenvalues[:, None]
    return jnp.real(jnp.fft.ifft(spectrum, axis=2)).astype(right_side.dtype)

def axial_rhs(shifted, row_index, line_length):
    interior = 0.5 * DERIV_NEAR * (shifted(1) - shifted(-1)) + 0.25 * DERIV_FAR * (shifted(2) - shifted(-2))
    row_opening = -2.5 * shifted(0) + 2.0 * shifted(1) + 0.5 * shifted(2)
    row_second = 0.75 * (shifted(1) - shifted(-1))
    row_closing = 2.5 * shifted(0) - 2.0 * shifted(-1) - 0.5 * shifted(-2)
    result = jnp.where(row_index == 0, row_opening, interior)
    result = jnp.where((row_index == 1) | (row_index == line_length - 2), row_second, result)
    return jnp.where(row_index == line_length - 1, row_closing, result)

def axial_bands(line_length, dtype):
    band_lower = jnp.full((line_length,), ALPHA_DERIV, dtype)
    band_lower = band_lower.at[0].set(0.0).at[1].set(0.25).at[line_length - 2].set(0.25).at[line_length - 1].set(2.0)
    band_middle = jnp.ones((line_length,), dtype)
    band_upper = jnp.full((line_length,), ALPHA_DERIV, dtype)
    band_upper = band_upper.at[0].set(2.0).at[1].set(0.25).at[line_length - 2].set(0.25).at[line_length - 1].set(0.0)
    return (band_lower, band_middle, band_upper)

def reference(fields):

    def circ_take(offset):
        return jnp.roll(fields, -offset, axis=2)
    circ_right = 0.5 * DERIV_NEAR * (circ_take(1) - circ_take(-1)) + 0.25 * DERIV_FAR * (circ_take(2) - circ_take(-2))
    terms = filter_terms(ALPHA_FILTER)
    filter_right = terms[0] * fields
    for offset in range(1, 6):
        filter_right = filter_right + 0.5 * terms[offset] * (circ_take(offset) + circ_take(-offset))
    deriv_circ = periodic_solve(circ_right, ALPHA_DERIV)
    filtered = periodic_solve(filter_right, ALPHA_FILTER)
    line_length = fields.shape[3]
    padded = jnp.pad(fields, ((0, 0), (0, 0), (0, 0), (2, 2)))

    def axial_take(offset):
        return padded[:, :, :, 2 + offset:2 + offset + line_length]
    row_index = jnp.arange(line_length)
    axial_right = axial_rhs(axial_take, row_index, line_length)
    band_lower, band_middle, band_upper = axial_bands(line_length, fields.dtype)
    band_shape = fields.shape[:2] + (line_length,)
    system = jnp.swapaxes(axial_right, 2, 3)
    solved = lax.linalg.tridiagonal_solve(jnp.broadcast_to(band_lower, band_shape), jnp.broadcast_to(band_middle, band_shape), jnp.broadcast_to(band_upper, band_shape), system)
    deriv_axial = jnp.swapaxes(solved, 2, 3)
    return (deriv_circ, deriv_axial, filtered)
```

```python
import functools
import math

import jax
import jax.numpy as jnp
import numpy as np
from jax import lax
from jax.experimental import pallas as pl
from jax.experimental.pallas import tpu as pltpu
from jax.sharding import PartitionSpec as P

DERIV_NEAR = 14.0 / 9.0
DERIV_FAR = 1.0 / 9.0
ALPHA_DERIV = 1.0 / 3.0
ALPHA_FILTER = 0.4999
PRECISE = lax.Precision.HIGHEST
REACH = 4


def filter_terms(coupling):
    return [
        (193.0 + 126.0 * coupling) / 256.0,
        (105.0 + 302.0 * coupling) / 256.0,
        15.0 * (2.0 * coupling - 1.0) / 64.0,
        45.0 * (1.0 - 2.0 * coupling) / 512.0,
        5.0 * (2.0 * coupling - 1.0) / 256.0,
        (1.0 - 2.0 * coupling) / 512.0,
    ]


def root_of(coupling):
    return (-1.0 + math.sqrt(1.0 - 4.0 * coupling * coupling)) / (2.0 * coupling)


def stencils():
    deriv = {
        1: 0.5 * DERIV_NEAR,
        -1: -0.5 * DERIV_NEAR,
        2: 0.25 * DERIV_FAR,
        -2: -0.25 * DERIV_FAR,
    }
    terms = filter_terms(ALPHA_FILTER)
    smooth = {0: terms[0]}
    for offset in range(1, 6):
        smooth[offset] = smooth[-offset] = 0.5 * terms[offset]
    return [(ALPHA_DERIV, deriv), (ALPHA_FILTER, smooth)]


def line_kernel(coupling, stencil):
    root = root_of(coupling)
    gain = 1.0 / (1.0 + 2.0 * coupling * root)

    def h(n):
        return gain * math.fsum(c * root ** abs(n + m) for m, c in stencil.items())

    right = gain * math.fsum(c * root**m for m, c in stencil.items())
    left = gain * math.fsum(c * root ** (-m) for m, c in stencil.items())
    return root, h, right, left


def circ_tables(cells):
    local = np.zeros((2, cells, cells))
    halo = np.zeros((2, cells, cells))
    for which, (coupling, stencil) in enumerate(stencils()):
        root, h, right, left = line_kernel(coupling, stencil)
        for i in range(cells):
            for k in range(cells):
                local[which, i, k] = h(i - k)
            for m in range(cells):
                n = i - (cells + m) if m < REACH else i - (m - cells)
                if 0 < abs(n) <= REACH:
                    halo[which, i, m] = h(n) - (right if n > 0 else left) * root ** abs(n)
    return local, halo


def carry_tables(cells, count):
    rounds = count.bit_length() - 1
    table = np.zeros((count, rounds + 1, 4))
    merge = np.zeros((rounds, 2))
    for which, (coupling, stencil) in enumerate(stencils()):
        root, _, right, left = line_kernel(coupling, stencil)
        step = root**cells
        wrap = 1.0 / (1.0 - step**count)
        for k in range(rounds):
            merge[k, which] = step ** (1 << k)
        for p in range(count):
            for k in range(rounds):
                size = 1 << k
                start = (p >> k) << k
                end = start + size - 1
                last = k == rounds - 1
                factor = wrap if last else 1.0
                if (p >> k) & 1:
                    table[p, k, 2 * which] = right * factor * step ** (p - start)
                    if last:
                        table[p, k, 2 * which + 1] = left * factor * step ** (count - 1 - p)
                else:
                    table[p, k, 2 * which + 1] = left * factor * step ** (end - p)
                    if last:
                        table[p, k, 2 * which] = right * factor * step**p
                if last:
                    table[p, rounds, 2 * which] = right * wrap * step ** (p + count - 1 - end)
                    table[p, rounds, 2 * which + 1] = left * wrap * step ** (start + count - 1 - p)
    return table, merge


def bands_table(line_length):
    band_lower = np.full(line_length, ALPHA_DERIV)
    band_lower[0] = 0.0
    band_lower[1] = 0.25
    band_lower[line_length - 2] = 0.25
    band_lower[line_length - 1] = 2.0
    band_upper = np.full(line_length, ALPHA_DERIV)
    band_upper[0] = 2.0
    band_upper[1] = 0.25
    band_upper[line_length - 2] = 0.25
    band_upper[line_length - 1] = 0.0
    return band_lower, band_upper


def axial_stencil(line_length):
    s = np.zeros((line_length, line_length))
    for k in range(2, line_length - 2):
        s[k, k + 1] = 0.5 * DERIV_NEAR
        s[k, k - 1] = -0.5 * DERIV_NEAR
        s[k, k + 2] = 0.25 * DERIV_FAR
        s[k, k - 2] = -0.25 * DERIV_FAR
    s[0, :3] = (-2.5, 2.0, 0.5)
    s[1, 0], s[1, 2] = -0.75, 0.75
    e = line_length - 1
    s[e - 1, e - 2], s[e - 1, e] = -0.75, 0.75
    s[e, e - 2 : e + 1] = (-0.5, -2.0, 2.5)
    return s


def axial_tables(line_cells, count):
    n = line_cells * count
    low, up = bands_table(n)
    s = axial_stencil(n)
    t = np.eye(n) + np.diag(low[1:], -1) + np.diag(up[:-1], 1)
    inverse = np.linalg.inv(t)
    full = inverse @ s
    from_top = np.zeros(n)
    from_top[0] = 1.0
    for i in range(1, n):
        from_top[i] = 1.0 - low[i] * up[i - 1] / from_top[i - 1]
    from_end = np.zeros(n)
    from_end[n - 1] = 1.0
    for i in range(n - 2, -1, -1):
        from_end[i] = 1.0 - up[i] * low[i + 1] / from_end[i + 1]
    down = -low / from_end
    back = -up / from_top
    local = np.zeros((count, line_cells, line_cells))
    gather = np.zeros((count, 4, line_cells))
    grow_down = np.zeros((count, line_cells))
    grow_back = np.zeros((count, line_cells))
    corner = np.zeros((count, 2))
    for p in range(count):
        b, e = p * line_cells, (p + 1) * line_cells
        local[p] = full[b:e, b:e]
        grow_down[p] = np.cumprod(down[b:e])
        grow_back[p] = np.cumprod(back[b:e][::-1])[::-1]
        gather[p, 2, 0] = 1.0
        gather[p, 3, line_cells - 1] = 1.0
        if e < n:
            y = inverse[e - 1].copy()
            y[e:] = 0.0
            for k in range(e, e + 2):
                y[k] = inverse[k, k] / np.prod(down[e : k + 1])
            gather[p, 0] = (y @ s)[b:e]
        if b > 0:
            y = inverse[b].copy()
            y[:b] = 0.0
            for k in range(b - 2, b):
                y[k] = inverse[k, k] / np.prod(back[k:b])
            gather[p, 1] = (y @ s)[b:e]
    for p in range(count):
        b, e = p * line_cells, (p + 1) * line_cells
        if p > 0:
            corner[p, 0] = full[b, b - 1] - grow_down[p, 0] * gather[p - 1, 0, -1]
        if p < count - 1:
            corner[p, 1] = full[e - 1, e] - grow_back[p, -1] * gather[p + 1, 1, 0]
    spread = np.zeros((count, count, 4, line_cells))
    for p in range(count):
        weight = 1.0
        for q in range(p - 1, -1, -1):
            spread[p, q, 0] = weight * grow_down[p]
            weight *= grow_down[q, -1]
        weight = 1.0
        for q in range(p + 1, count):
            spread[p, q, 1] = weight * grow_back[p]
            weight *= grow_back[q, 0]
        if p > 0:
            spread[p, p - 1, 3, 0] = corner[p, 0]
        if p < count - 1:
            spread[p, p + 1, 2, -1] = corner[p, 1]
    return local, gather, spread


def by_row(values, shape):
    rows = lax.broadcasted_iota(jnp.int32, shape, len(shape) - 2)
    out = jnp.full(shape, float(values[0]), jnp.float32)
    for i in range(1, len(values)):
        out = jnp.where(rows == i, jnp.float32(values[i]), out)
    return out


def totals_kernel(weights, u_ref, s_ref, first_ref, last_ref):
    lines, cells, width = u_ref.shape
    w = [by_row(weights[v], (cells, width)) for v in range(4)]
    for n in range(lines):
        un = u_ref[n]
        for v in range(4):
            s_ref[v, n : n + 1, :] = jnp.sum(un * w[v], axis=0, keepdims=True)
        first_ref[n] = un[:REACH]
        last_ref[n] = un[cells - REACH :]


def near_kernel(local, halo, u_ref, right_ref, left_ref, d_ref, f_ref):
    lines, cells, width = u_ref.shape
    outs = (d_ref, f_ref)
    diag = {}
    for name, table in (("local", local), ("halo", halo)):
        for which in range(2):
            for s in range(cells):
                values = [table[which, i, (i - s) % cells] for i in range(cells)]
                if np.any(np.asarray(values) != 0.0):
                    diag[name, which, s] = by_row(values, (cells, width))
    for n in range(lines):
        un = u_ref[n]
        hn = jnp.concatenate([right_ref[n], left_ref[n]], axis=0)
        acc = [None, None]
        for name, value in (("local", un), ("halo", hn)):
            for s in range(cells):
                used = [w for w in range(2) if (name, w, s) in diag]
                if not used:
                    continue
                turned = pltpu.roll(value, s, 0) if s else value
                for w in used:
                    term = turned * diag[name, w, s]
                    acc[w] = term if acc[w] is None else acc[w] + term
        for w in range(2):
            outs[w][n] = acc[w]


def far_kernel(rounds, roots, coef_ref, *refs):
    got = refs[: rounds + 1]
    d_near, f_near, d_ref, f_ref, lr = refs[rounds + 1 :]
    lines, cells, width = d_near.shape
    for v in range(4):
        total = got[0][v] * coef_ref[0, v]
        for k in range(1, rounds + 1):
            total = total + got[k][v] * coef_ref[k, v]
        lr[v] = total
    near = (d_near, f_near)
    outs = (d_ref, f_ref)
    for which in range(2):
        a = by_row([roots[which] ** (i + 1) for i in range(cells)], (cells, width))
        b = by_row([roots[which] ** (cells - i) for i in range(cells)], (cells, width))
        for n in range(lines):
            from_left = jnp.broadcast_to(lr[2 * which, n : n + 1, :], (cells, width))
            from_right = jnp.broadcast_to(lr[2 * which + 1, n : n + 1, :], (cells, width))
            outs[which][n] = near[which][n] + a * from_left + b * from_right


def vmem(count):
    return [pl.BlockSpec(memory_space=pltpu.VMEM)] * count


def shards(fields):
    parts, radial, cells, width = fields.shape
    lines = parts * radial
    u = fields.reshape(lines, cells, width)
    circ_count = lax.axis_size("circ")
    circ_place = lax.axis_index("circ")
    ax_count = lax.axis_size("ax")
    ax_place = lax.axis_index("ax")
    rounds = circ_count.bit_length() - 1
    roots = [root_of(ALPHA_DERIV), root_of(ALPHA_FILTER)]
    f32 = jnp.float32

    weights = np.zeros((4, cells))
    for which, root in enumerate(roots):
        weights[2 * which] = root ** (cells - 1.0 - np.arange(cells))
        weights[2 * which + 1] = root ** (1.0 * np.arange(cells))
    totals, first, last = pl.pallas_call(
        functools.partial(totals_kernel, weights),
        out_shape=(
            jax.ShapeDtypeStruct((4, lines, width), f32),
            jax.ShapeDtypeStruct((lines, REACH, width), f32),
            jax.ShapeDtypeStruct((lines, REACH, width), f32),
        ),
        in_specs=vmem(1),
        out_specs=tuple(vmem(3)),
        name="totals",
    )(u)

    table, merge = carry_tables(cells, circ_count)
    coef = lax.dynamic_index_in_dim(jnp.asarray(table, f32), circ_place, 0, False)
    masks = [1, 3, 4, 8, 16, 48]
    got = []
    for k in range(rounds):
        other = lax.ppermute(totals, "circ", [(i, i ^ masks[k]) for i in range(circ_count)])
        got.append(other)
        if k < rounds - 1:
            on_right = ((circ_place >> k) & 1) == 1
            grow = [float(merge[k, 0]), float(merge[k, 1])]
            own, their = [], []
            for which in range(2):
                one = jnp.float32(1.0)
                g = jnp.float32(grow[which])
                own += [jnp.where(on_right, one, g), jnp.where(on_right, g, one)]
                their += [jnp.where(on_right, g, one), jnp.where(on_right, one, g)]
            totals = jnp.stack([own[v] * totals[v] + their[v] * other[v] for v in range(4)])
    got.append(totals)

    ring = [(i, (i + 1) % circ_count) for i in range(circ_count)]
    gnir = [(j, i) for i, j in ring]
    left = lax.ppermute(last, "circ", ring)
    right = lax.ppermute(first, "circ", gnir)

    local, halo = circ_tables(cells)
    d_near, f_near = pl.pallas_call(
        functools.partial(near_kernel, local, halo),
        out_shape=(jax.ShapeDtypeStruct(u.shape, f32),) * 2,
        in_specs=vmem(3),
        out_specs=tuple(vmem(2)),
        name="near",
    )(u, right, left)

    ax_local, ax_gather, ax_spread = axial_tables(width, ax_count)
    rows = u.reshape(lines * cells, width)
    mine = lax.dynamic_index_in_dim(jnp.asarray(ax_gather, f32), ax_place, 0, False)
    sent = lax.dot_general(mine, rows, (((1,), (1,)), ((), ())), precision=PRECISE)
    near_side = lax.ppermute(sent, "ax", [(i, i ^ 1) for i in range(ax_count)])
    pair = jnp.concatenate([sent, near_side], axis=0)
    far_side = lax.ppermute(pair, "ax", [(i, i ^ 2) for i in range(ax_count)])
    order = np.asarray([[p ^ 1, p ^ 2, p ^ 3] for p in range(ax_count)])
    spread = np.stack([ax_spread[p][order[p]].reshape(12, width) for p in range(ax_count)])
    spread = lax.dynamic_index_in_dim(jnp.asarray(spread, f32), ax_place, 0, False)
    square = lax.dynamic_index_in_dim(jnp.asarray(ax_local.swapaxes(1, 2), f32), ax_place, 0, False)
    ax_in = jnp.concatenate([near_side, far_side], axis=0)
    ax_out = jnp.dot(rows, square, precision=PRECISE)
    ax_out = ax_out + lax.dot_general(ax_in, spread, (((0,), (0,)), ((), ())), precision=PRECISE)

    d_circ, filtered = pl.pallas_call(
        functools.partial(far_kernel, rounds, roots),
        out_shape=(jax.ShapeDtypeStruct(u.shape, f32),) * 2,
        in_specs=[pl.BlockSpec(memory_space=pltpu.SMEM)] + vmem(rounds + 3),
        out_specs=tuple(vmem(2)),
        scratch_shapes=[pltpu.VMEM((4, lines, width), f32)],
        name="far",
    )(coef, *got, d_near, f_near)
    shape = fields.shape
    return d_circ.reshape(shape), ax_out.reshape(shape), filtered.reshape(shape)


def solution(mesh):
    spec = P(None, None, "circ", "ax")
    return jax.shard_map(
        shards, mesh=mesh, in_specs=(spec,), out_specs=(spec, spec, spec), check_vma=False
    )
```

```python
import functools
import math

import jax
import jax.numpy as jnp
import numpy as np
from jax import lax
from jax.experimental import pallas as pl
from jax.experimental.pallas import tpu as pltpu
from jax.sharding import PartitionSpec as P

DERIV_NEAR = 14.0 / 9.0
DERIV_FAR = 1.0 / 9.0
ALPHA_DERIV = 1.0 / 3.0
ALPHA_FILTER = 0.4999
PRECISE = lax.Precision.HIGHEST
REACH = 4


def filter_terms(coupling):
    return [
        (193.0 + 126.0 * coupling) / 256.0,
        (105.0 + 302.0 * coupling) / 256.0,
        15.0 * (2.0 * coupling - 1.0) / 64.0,
        45.0 * (1.0 - 2.0 * coupling) / 512.0,
        5.0 * (2.0 * coupling - 1.0) / 256.0,
        (1.0 - 2.0 * coupling) / 512.0,
    ]


def root_of(coupling):
    return (-1.0 + math.sqrt(1.0 - 4.0 * coupling * coupling)) / (2.0 * coupling)


def stencils():
    deriv = {
        1: 0.5 * DERIV_NEAR,
        -1: -0.5 * DERIV_NEAR,
        2: 0.25 * DERIV_FAR,
        -2: -0.25 * DERIV_FAR,
    }
    terms = filter_terms(ALPHA_FILTER)
    smooth = {0: terms[0]}
    for offset in range(1, 6):
        smooth[offset] = smooth[-offset] = 0.5 * terms[offset]
    return [(ALPHA_DERIV, deriv), (ALPHA_FILTER, smooth)]


def line_kernel(coupling, stencil):
    root = root_of(coupling)
    gain = 1.0 / (1.0 + 2.0 * coupling * root)

    def h(n):
        return gain * math.fsum(c * root ** abs(n + m) for m, c in stencil.items())

    right = gain * math.fsum(c * root**m for m, c in stencil.items())
    left = gain * math.fsum(c * root ** (-m) for m, c in stencil.items())
    return root, h, right, left


def circ_tables(cells):
    local = np.zeros((2, cells, cells))
    halo = np.zeros((2, cells, cells))
    for which, (coupling, stencil) in enumerate(stencils()):
        root, h, right, left = line_kernel(coupling, stencil)
        for i in range(cells):
            for k in range(cells):
                local[which, i, k] = h(i - k)
            for m in range(cells):
                n = i - (cells + m) if m < REACH else i - (m - cells)
                if 0 < abs(n) <= REACH:
                    halo[which, i, m] = h(n) - (right if n > 0 else left) * root ** abs(n)
    return local, halo


def carry_tables(cells, count):
    rounds = count.bit_length() - 1
    table = np.zeros((count, rounds + 1, 4))
    merge = np.zeros((rounds, 2))
    for which, (coupling, stencil) in enumerate(stencils()):
        root, _, right, left = line_kernel(coupling, stencil)
        step = root**cells
        wrap = 1.0 / (1.0 - step**count)
        for k in range(rounds):
            merge[k, which] = step ** (1 << k)
        for p in range(count):
            for k in range(rounds):
                size = 1 << k
                start = (p >> k) << k
                end = start + size - 1
                last = k == rounds - 1
                factor = wrap if last else 1.0
                if (p >> k) & 1:
                    table[p, k, 2 * which] = right * factor * step ** (p - start)
                    if last:
                        table[p, k, 2 * which + 1] = left * factor * step ** (count - 1 - p)
                else:
                    table[p, k, 2 * which + 1] = left * factor * step ** (end - p)
                    if last:
                        table[p, k, 2 * which] = right * factor * step**p
                if last:
                    table[p, rounds, 2 * which] = right * wrap * step ** (p + count - 1 - end)
                    table[p, rounds, 2 * which + 1] = left * wrap * step ** (start + count - 1 - p)
    return table, merge


def bands_table(line_length):
    band_lower = np.full(line_length, ALPHA_DERIV)
    band_lower[0] = 0.0
    band_lower[1] = 0.25
    band_lower[line_length - 2] = 0.25
    band_lower[line_length - 1] = 2.0
    band_upper = np.full(line_length, ALPHA_DERIV)
    band_upper[0] = 2.0
    band_upper[1] = 0.25
    band_upper[line_length - 2] = 0.25
    band_upper[line_length - 1] = 0.0
    return band_lower, band_upper


def axial_stencil(line_length):
    s = np.zeros((line_length, line_length))
    for k in range(2, line_length - 2):
        s[k, k + 1] = 0.5 * DERIV_NEAR
        s[k, k - 1] = -0.5 * DERIV_NEAR
        s[k, k + 2] = 0.25 * DERIV_FAR
        s[k, k - 2] = -0.25 * DERIV_FAR
    s[0, :3] = (-2.5, 2.0, 0.5)
    s[1, 0], s[1, 2] = -0.75, 0.75
    e = line_length - 1
    s[e - 1, e - 2], s[e - 1, e] = -0.75, 0.75
    s[e, e - 2 : e + 1] = (-0.5, -2.0, 2.5)
    return s


def axial_tables(line_cells, count):
    n = line_cells * count
    low, up = bands_table(n)
    s = axial_stencil(n)
    t = np.eye(n) + np.diag(low[1:], -1) + np.diag(up[:-1], 1)
    inverse = np.linalg.inv(t)
    full = inverse @ s
    from_top = np.zeros(n)
    from_top[0] = 1.0
    for i in range(1, n):
        from_top[i] = 1.0 - low[i] * up[i - 1] / from_top[i - 1]
    from_end = np.zeros(n)
    from_end[n - 1] = 1.0
    for i in range(n - 2, -1, -1):
        from_end[i] = 1.0 - up[i] * low[i + 1] / from_end[i + 1]
    down = -low / from_end
    back = -up / from_top
    local = np.zeros((count, line_cells, line_cells))
    gather = np.zeros((count, 4, line_cells))
    grow_down = np.zeros((count, line_cells))
    grow_back = np.zeros((count, line_cells))
    corner = np.zeros((count, 2))
    for p in range(count):
        b, e = p * line_cells, (p + 1) * line_cells
        local[p] = full[b:e, b:e]
        grow_down[p] = np.cumprod(down[b:e])
        grow_back[p] = np.cumprod(back[b:e][::-1])[::-1]
        gather[p, 2, 0] = 1.0
        gather[p, 3, line_cells - 1] = 1.0
        if e < n:
            y = inverse[e - 1].copy()
            y[e:] = 0.0
            for k in range(e, e + 2):
                y[k] = inverse[k, k] / np.prod(down[e : k + 1])
            gather[p, 0] = (y @ s)[b:e]
        if b > 0:
            y = inverse[b].copy()
            y[:b] = 0.0
            for k in range(b - 2, b):
                y[k] = inverse[k, k] / np.prod(back[k:b])
            gather[p, 1] = (y @ s)[b:e]
    for p in range(count):
        b, e = p * line_cells, (p + 1) * line_cells
        if p > 0:
            corner[p, 0] = full[b, b - 1] - grow_down[p, 0] * gather[p - 1, 0, -1]
        if p < count - 1:
            corner[p, 1] = full[e - 1, e] - grow_back[p, -1] * gather[p + 1, 1, 0]
    spread = np.zeros((count, count, 4, line_cells))
    for p in range(count):
        weight = 1.0
        for q in range(p - 1, -1, -1):
            spread[p, q, 0] = weight * grow_down[p]
            weight *= grow_down[q, -1]
        weight = 1.0
        for q in range(p + 1, count):
            spread[p, q, 1] = weight * grow_back[p]
            weight *= grow_back[q, 0]
        if p > 0:
            spread[p, p - 1, 3, 0] = corner[p, 0]
        if p < count - 1:
            spread[p, p + 1, 2, -1] = corner[p, 1]
    return local, gather, spread


def by_row(values, shape):
    rows = lax.broadcasted_iota(jnp.int32, shape, len(shape) - 2)
    out = jnp.full(shape, float(values[0]), jnp.float32)
    for i in range(1, len(values)):
        out = jnp.where(rows == i, jnp.float32(values[i]), out)
    return out


def totals_kernel(weights, u_ref, s_ref, first_ref, last_ref):
    lines, cells, width = u_ref.shape
    w = [by_row(weights[v], (cells, width)) for v in range(4)]
    for n in range(lines):
        un = u_ref[n]
        for v in range(4):
            s_ref[v, n : n + 1, :] = jnp.sum(un * w[v], axis=0, keepdims=True)
        first_ref[n] = un[:REACH]
        last_ref[n] = un[cells - REACH :]


def near_kernel(local, halo, u_ref, right_ref, left_ref, d_ref, f_ref):
    lines, cells, width = u_ref.shape
    outs = (d_ref, f_ref)
    diag = {}
    for name, table in (("local", local), ("halo", halo)):
        for which in range(2):
            for s in range(cells):
                values = [table[which, i, (i - s) % cells] for i in range(cells)]
                if np.any(np.asarray(values) != 0.0):
                    diag[name, which, s] = by_row(values, (cells, width))
    for n in range(lines):
        un = u_ref[n]
        hn = jnp.concatenate([right_ref[n], left_ref[n]], axis=0)
        acc = [None, None]
        for name, value in (("local", un), ("halo", hn)):
            for s in range(cells):
                used = [w for w in range(2) if (name, w, s) in diag]
                if not used:
                    continue
                turned = pltpu.roll(value, s, 0) if s else value
                for w in used:
                    term = turned * diag[name, w, s]
                    acc[w] = term if acc[w] is None else acc[w] + term
        for w in range(2):
            outs[w][n] = acc[w]


def far_kernel(rounds, roots, coef_ref, *refs):
    got = refs[: rounds + 1]
    d_near, f_near, d_ref, f_ref, lr = refs[rounds + 1 :]
    lines, cells, width = d_near.shape
    for v in range(4):
        total = got[0][v] * coef_ref[0, v]
        for k in range(1, rounds + 1):
            total = total + got[k][v] * coef_ref[k, v]
        lr[v] = total
    near = (d_near, f_near)
    outs = (d_ref, f_ref)
    for which in range(2):
        a = by_row([roots[which] ** (i + 1) for i in range(cells)], (cells, width))
        b = by_row([roots[which] ** (cells - i) for i in range(cells)], (cells, width))
        for n in range(lines):
            from_left = jnp.broadcast_to(lr[2 * which, n : n + 1, :], (cells, width))
            from_right = jnp.broadcast_to(lr[2 * which + 1, n : n + 1, :], (cells, width))
            outs[which][n] = near[which][n] + a * from_left + b * from_right


def in_vmem(x):
    return pltpu.with_memory_space_constraint(x, pltpu.VMEM)


def vmem(count):
    return [pl.BlockSpec(memory_space=pltpu.VMEM)] * count


def shards(fields):
    parts, radial, cells, width = fields.shape
    lines = parts * radial
    u = fields.reshape(lines, cells, width)
    circ_count = lax.axis_size("circ")
    circ_place = lax.axis_index("circ")
    ax_count = lax.axis_size("ax")
    ax_place = lax.axis_index("ax")
    rounds = circ_count.bit_length() - 1
    roots = [root_of(ALPHA_DERIV), root_of(ALPHA_FILTER)]
    f32 = jnp.float32

    weights = np.zeros((4, cells))
    for which, root in enumerate(roots):
        weights[2 * which] = root ** (cells - 1.0 - np.arange(cells))
        weights[2 * which + 1] = root ** (1.0 * np.arange(cells))
    totals, first, last = pl.pallas_call(
        functools.partial(totals_kernel, weights),
        out_shape=(
            pltpu.VMEM((4, lines, width), f32),
            pltpu.VMEM((lines, REACH, width), f32),
            pltpu.VMEM((lines, REACH, width), f32),
        ),
        in_specs=vmem(1),
        out_specs=tuple(vmem(3)),
        name="totals",
    )(u)

    table, merge = carry_tables(cells, circ_count)
    coef = lax.dynamic_index_in_dim(jnp.asarray(table, f32), circ_place, 0, False)
    masks = [1, 3, 4, 8, 16, 48]
    got = []
    for k in range(rounds):
        other = lax.ppermute(totals, "circ", [(i, i ^ masks[k]) for i in range(circ_count)])
        got.append(other)
        if k < rounds - 1:
            on_right = ((circ_place >> k) & 1) == 1
            grow = [float(merge[k, 0]), float(merge[k, 1])]
            own, their = [], []
            for which in range(2):
                one = jnp.float32(1.0)
                g = jnp.float32(grow[which])
                own += [jnp.where(on_right, one, g), jnp.where(on_right, g, one)]
                their += [jnp.where(on_right, g, one), jnp.where(on_right, one, g)]
            totals = jnp.stack([own[v] * totals[v] + their[v] * other[v] for v in range(4)])
    got.append(totals)

    ring = [(i, (i + 1) % circ_count) for i in range(circ_count)]
    gnir = [(j, i) for i, j in ring]
    left = lax.ppermute(last, "circ", ring)
    right = lax.ppermute(first, "circ", gnir)

    local, halo = circ_tables(cells)
    d_near, f_near = pl.pallas_call(
        functools.partial(near_kernel, local, halo),
        out_shape=(pltpu.VMEM(u.shape, f32),) * 2,
        in_specs=vmem(3),
        out_specs=tuple(vmem(2)),
        name="near",
    )(u, in_vmem(right), in_vmem(left))

    ax_local, ax_gather, ax_spread = axial_tables(width, ax_count)
    rows = u.reshape(lines * cells, width)
    mine = lax.dynamic_index_in_dim(jnp.asarray(ax_gather, f32), ax_place, 0, False)
    sent = lax.dot_general(mine, rows, (((1,), (1,)), ((), ())), precision=PRECISE)
    near_side = lax.ppermute(sent, "ax", [(i, i ^ 1) for i in range(ax_count)])
    pair = jnp.concatenate([sent, near_side], axis=0)
    far_side = lax.ppermute(pair, "ax", [(i, i ^ 2) for i in range(ax_count)])
    order = np.asarray([[p ^ 1, p ^ 2, p ^ 3] for p in range(ax_count)])
    spread = np.stack([ax_spread[p][order[p]].reshape(12, width) for p in range(ax_count)])
    spread = lax.dynamic_index_in_dim(jnp.asarray(spread, f32), ax_place, 0, False)
    square = lax.dynamic_index_in_dim(jnp.asarray(ax_local.swapaxes(1, 2), f32), ax_place, 0, False)
    ax_in = jnp.concatenate([near_side, far_side], axis=0)
    ax_out = jnp.dot(rows, square, precision=PRECISE)
    ax_out = ax_out + lax.dot_general(ax_in, spread, (((0,), (0,)), ((), ())), precision=PRECISE)

    d_circ, filtered = pl.pallas_call(
        functools.partial(far_kernel, rounds, roots),
        out_shape=(jax.ShapeDtypeStruct(u.shape, f32),) * 2,
        in_specs=[pl.BlockSpec(memory_space=pltpu.SMEM)] + vmem(rounds + 3),
        out_specs=tuple(vmem(2)),
        scratch_shapes=[pltpu.VMEM((4, lines, width), f32)],
        name="far",
    )(coef, *[in_vmem(x) for x in got], in_vmem(d_near), in_vmem(f_near))
    shape = fields.shape
    return d_circ.reshape(shape), ax_out.reshape(shape), filtered.reshape(shape)


def solution(mesh):
    spec = P(None, None, "circ", "ax")
    return jax.shard_map(
        shards, mesh=mesh, in_specs=(spec,), out_specs=(spec, spec, spec), check_vma=False
    )
```

```python
import functools
import math

import jax
import jax.numpy as jnp
import numpy as np
from jax import lax
from jax.experimental import pallas as pl
from jax.experimental.pallas import tpu as pltpu
from jax.sharding import PartitionSpec as P


DERIV_NEAR = 14.0 / 9.0
DERIV_FAR = 1.0 / 9.0
ALPHA_DERIV = 1.0 / 3.0
ALPHA_FILTER = 0.4999
PRECISE = lax.Precision.HIGHEST
REACH = 4
CHUNKS = 4
GROUP = 4


def filter_terms(coupling):
    return [
        (193.0 + 126.0 * coupling) / 256.0,
        (105.0 + 302.0 * coupling) / 256.0,
        15.0 * (2.0 * coupling - 1.0) / 64.0,
        45.0 * (1.0 - 2.0 * coupling) / 512.0,
        5.0 * (2.0 * coupling - 1.0) / 256.0,
        (1.0 - 2.0 * coupling) / 512.0,
    ]


def root_of(coupling):
    return (-1.0 + math.sqrt(1.0 - 4.0 * coupling * coupling)) / (2.0 * coupling)


def stencils():
    deriv = {
        1: 0.5 * DERIV_NEAR,
        -1: -0.5 * DERIV_NEAR,
        2: 0.25 * DERIV_FAR,
        -2: -0.25 * DERIV_FAR,
    }
    terms = filter_terms(ALPHA_FILTER)
    smooth = {0: terms[0]}
    for offset in range(1, 6):
        smooth[offset] = smooth[-offset] = 0.5 * terms[offset]
    return [(ALPHA_DERIV, deriv), (ALPHA_FILTER, smooth)]


def line_kernel(coupling, stencil):
    root = root_of(coupling)
    gain = 1.0 / (1.0 + 2.0 * coupling * root)

    def h(n):
        return gain * math.fsum(c * root ** abs(n + m) for m, c in stencil.items())

    right = gain * math.fsum(c * root**m for m, c in stencil.items())
    left = gain * math.fsum(c * root ** (-m) for m, c in stencil.items())
    return root, h, right, left


def circ_tables(cells):
    local = np.zeros((2, cells, cells))
    halo = np.zeros((2, cells, cells))
    for which, (coupling, stencil) in enumerate(stencils()):
        root, h, right, left = line_kernel(coupling, stencil)
        for i in range(cells):
            for k in range(cells):
                local[which, i, k] = h(i - k)
            for m in range(cells):
                n = i - (cells + m) if m < REACH else i - (m - cells)
                if 0 < abs(n) <= REACH:
                    halo[which, i, m] = h(n) - (right if n > 0 else left) * root ** abs(n)
    return local, halo


def carry_tables(cells, count, group):
    first = group.bit_length() - 1
    rounds = count.bit_length() - 1
    later = rounds - first
    table = np.zeros((count, group - 1 + later + 1, 4))
    merge = np.zeros((rounds, 2))
    for which, (coupling, stencil) in enumerate(stencils()):
        root, _, right, left = line_kernel(coupling, stencil)
        step = root**cells
        wrap = 1.0 / (1.0 - step**count)
        for k in range(rounds):
            merge[k, which] = step ** (1 << k)
        for p in range(count):
            rows = table[p, :, 2 * which : 2 * which + 2]
            for m in range(1, group):
                q = p ^ m
                if q < p:
                    rows[m - 1, 0] = right * step ** (p - q - 1)
                else:
                    rows[m - 1, 1] = left * step ** (q - p - 1)
            for k in range(first, rounds):
                start = (p >> k) << k
                end = start + (1 << k) - 1
                last = k == rounds - 1
                slot = group - 1 + k - first + (1 if last else 0)
                factor = wrap if last else 1.0
                upper = (p >> k) & 1
                if upper or last:
                    rows[slot, 0] = right * factor * step ** (p - start if upper else p)
                if not upper or last:
                    rows[slot, 1] = left * factor * step ** (count - 1 - p if upper else end - p)
                if last:
                    rows[slot - 1, 0] = right * wrap * step ** (p + count - 1 - end)
                    rows[slot - 1, 1] = left * wrap * step ** (start + count - 1 - p)
    return table, merge


def bands_table(line_length):
    band_lower = np.full(line_length, ALPHA_DERIV)
    band_lower[0] = 0.0
    band_lower[1] = 0.25
    band_lower[line_length - 2] = 0.25
    band_lower[line_length - 1] = 2.0
    band_upper = np.full(line_length, ALPHA_DERIV)
    band_upper[0] = 2.0
    band_upper[1] = 0.25
    band_upper[line_length - 2] = 0.25
    band_upper[line_length - 1] = 0.0
    return band_lower, band_upper


def axial_stencil(line_length):
    s = np.zeros((line_length, line_length))
    for k in range(2, line_length - 2):
        s[k, k + 1] = 0.5 * DERIV_NEAR
        s[k, k - 1] = -0.5 * DERIV_NEAR
        s[k, k + 2] = 0.25 * DERIV_FAR
        s[k, k - 2] = -0.25 * DERIV_FAR
    s[0, :3] = (-2.5, 2.0, 0.5)
    s[1, 0], s[1, 2] = -0.75, 0.75
    e = line_length - 1
    s[e - 1, e - 2], s[e - 1, e] = -0.75, 0.75
    s[e, e - 2 : e + 1] = (-0.5, -2.0, 2.5)
    return s


def axial_tables(line_cells, count):
    n = line_cells * count
    low, up = bands_table(n)
    s = axial_stencil(n)
    t = np.eye(n) + np.diag(low[1:], -1) + np.diag(up[:-1], 1)
    inverse = np.linalg.inv(t)
    full = inverse @ s
    from_top = np.zeros(n)
    from_top[0] = 1.0
    for i in range(1, n):
        from_top[i] = 1.0 - low[i] * up[i - 1] / from_top[i - 1]
    from_end = np.zeros(n)
    from_end[n - 1] = 1.0
    for i in range(n - 2, -1, -1):
        from_end[i] = 1.0 - up[i] * low[i + 1] / from_end[i + 1]
    down = -low / from_end
    back = -up / from_top
    local = np.zeros((count, line_cells, line_cells))
    gather = np.zeros((count, 4, line_cells))
    grow_down = np.zeros((count, line_cells))
    grow_back = np.zeros((count, line_cells))
    corner = np.zeros((count, 2))
    for p in range(count):
        b, e = p * line_cells, (p + 1) * line_cells
        local[p] = full[b:e, b:e]
        grow_down[p] = np.cumprod(down[b:e])
        grow_back[p] = np.cumprod(back[b:e][::-1])[::-1]
        gather[p, 2, 0] = 1.0
        gather[p, 3, line_cells - 1] = 1.0
        if e < n:
            y = inverse[e - 1].copy()
            y[e:] = 0.0
            for k in range(e, e + 2):
                y[k] = inverse[k, k] / np.prod(down[e : k + 1])
            gather[p, 0] = (y @ s)[b:e]
        if b > 0:
            y = inverse[b].copy()
            y[:b] = 0.0
            for k in range(b - 2, b):
                y[k] = inverse[k, k] / np.prod(back[k:b])
            gather[p, 1] = (y @ s)[b:e]
    for p in range(count):
        b, e = p * line_cells, (p + 1) * line_cells
        if p > 0:
            corner[p, 0] = full[b, b - 1] - grow_down[p, 0] * gather[p - 1, 0, -1]
        if p < count - 1:
            corner[p, 1] = full[e - 1, e] - grow_back[p, -1] * gather[p + 1, 1, 0]
    spread = np.zeros((count, count, 4, line_cells))
    for p in range(count):
        weight = 1.0
        for q in range(p - 1, -1, -1):
            spread[p, q, 0] = weight * grow_down[p]
            weight *= grow_down[q, -1]
        weight = 1.0
        for q in range(p + 1, count):
            spread[p, q, 1] = weight * grow_back[p]
            weight *= grow_back[q, 0]
        if p > 0:
            spread[p, p - 1, 3, 0] = corner[p, 0]
        if p < count - 1:
            spread[p, p + 1, 2, -1] = corner[p, 1]
    return local, gather, spread


def by_row(values, shape):
    rows = lax.broadcasted_iota(jnp.int32, shape, len(shape) - 2)
    out = jnp.full(shape, float(values[0]), jnp.float32)
    for i in range(1, len(values)):
        out = jnp.where(rows == i, jnp.float32(values[i]), out)
    return out


def totals_kernel(weights, u_hbm, s_ref, u_ref, sems):
    lines, cells, width = u_ref.shape
    chunk = lines // CHUNKS
    copies = []
    for c in range(CHUNKS):
        part = pl.ds(c * chunk, chunk)
        copies.append(pltpu.make_async_copy(u_hbm.at[part], u_ref.at[part], sems.at[c]))
        copies[-1].start()
    w = [by_row(weights[v], (cells, width)) for v in range(4)]
    for c in range(CHUNKS):
        copies[c].wait()
        for n in range(c * chunk, (c + 1) * chunk):
            un = u_ref[n]
            for v in range(4):
                s_ref[v, n : n + 1, :] = jnp.sum(un * w[v], axis=0, keepdims=True)


def edges_kernel(u_ref, first_ref, last_ref):
    lines, cells, _ = u_ref.shape
    for n in range(lines):
        un = u_ref[n]
        first_ref[n] = un[:REACH]
        last_ref[n] = un[cells - REACH :]


def near_kernel(local, halo, count, roots, coef_ref, u_ref, right_ref, left_ref, *refs):
    got = refs[:count]
    d_ref, f_ref, tile_ref, lr = refs[count:]
    lines, cells, width = u_ref.shape
    outs = (d_ref, f_ref)
    for v in range(4):
        total = got[0][v] * coef_ref[0, v]
        for k in range(1, count):
            total = total + got[k][v] * coef_ref[k, v]
        lr[v] = total
        tile_ref[v] = jnp.full(tile_ref.shape[1:], coef_ref[count, v], jnp.float32)
    diag = {}
    for name, table in (("local", local), ("halo", halo)):
        for which in range(2):
            for s in range(cells):
                values = [table[which, i, (i - s) % cells] for i in range(cells)]
                if np.any(np.asarray(values) != 0.0):
                    diag[name, which, s] = by_row(values, (cells, width))
    ramps = ramp_rows(roots, cells, width)
    for n in range(lines):
        un = u_ref[n]
        hn = jnp.concatenate([right_ref[n], left_ref[n]], axis=0)
        acc = [
            ramps[2 * w] * jnp.broadcast_to(lr[2 * w, n : n + 1, :], (cells, width))
            + ramps[2 * w + 1] * jnp.broadcast_to(lr[2 * w + 1, n : n + 1, :], (cells, width))
            for w in range(2)
        ]
        for name, value in (("local", un), ("halo", hn)):
            for s in range(cells):
                used = [w for w in range(2) if (name, w, s) in diag]
                if not used:
                    continue
                turned = pltpu.roll(value, s, 0) if s else value
                for w in used:
                    acc[w] = acc[w] + turned * diag[name, w, s]
        for w in range(2):
            outs[w][n] = acc[w]


def ramp_rows(roots, cells, width):
    out = []
    for root in roots:
        out.append(by_row([root ** (i + 1) for i in range(cells)], (cells, width)))
        out.append(by_row([root ** (cells - i) for i in range(cells)], (cells, width)))
    return out


def far_kernel(roots, tile_ref, got, d_near, f_near, d_hbm, f_hbm, lr, done, sems):
    lines, cells, width = d_near.shape
    chunk = lines // CHUNKS
    ramps = ramp_rows(roots, cells, width)
    near = (d_near, f_near)
    hbm = (d_hbm, f_hbm)
    for v in range(4):
        for n in range(0, lines, 8):
            lr[v, n : n + 8] = got[v, n : n + 8] * tile_ref[v]
    copies = []
    for c in range(CHUNKS):
        part = pl.ds(c * chunk, chunk)
        for w in range(2):
            for n in range(c * chunk, (c + 1) * chunk):
                from_left = jnp.broadcast_to(lr[2 * w, n : n + 1, :], (cells, width))
                from_right = jnp.broadcast_to(lr[2 * w + 1, n : n + 1, :], (cells, width))
                done[w, n] = (
                    near[w][n] + ramps[2 * w] * from_left + ramps[2 * w + 1] * from_right
                )
            copies.append(
                pltpu.make_async_copy(done.at[w, part], hbm[w].at[part], sems.at[w, c])
            )
            copies[-1].start()
    for copy in copies:
        copy.wait()


def in_vmem(x):
    return pltpu.with_memory_space_constraint(x, pltpu.VMEM)


def vmem(count):
    return [pl.BlockSpec(memory_space=pltpu.VMEM)] * count


def shards(fields):
    parts, radial, cells, width = fields.shape
    lines = parts * radial
    u = fields.reshape(lines, cells, width)
    circ_count = lax.axis_size("circ")
    circ_place = lax.axis_index("circ")
    ax_count = lax.axis_size("ax")
    ax_place = lax.axis_index("ax")
    rounds = circ_count.bit_length() - 1
    roots = [root_of(ALPHA_DERIV), root_of(ALPHA_FILTER)]
    f32 = jnp.float32

    weights = np.zeros((4, cells))
    for which, root in enumerate(roots):
        weights[2 * which] = root ** (cells - 1.0 - np.arange(cells))
        weights[2 * which + 1] = root ** (1.0 * np.arange(cells))
    totals, u = pl.pallas_call(
        functools.partial(totals_kernel, weights),
        out_shape=(pltpu.VMEM((4, lines, width), f32), pltpu.VMEM(u.shape, f32)),
        in_specs=[pl.BlockSpec(memory_space=pl.ANY)],
        out_specs=tuple(vmem(2)),
        scratch_shapes=[pltpu.SemaphoreType.DMA((CHUNKS,))],
        name="totals",
    )(u)

    table, merge = carry_tables(cells, circ_count, GROUP)
    steps = [root**cells for root in roots]
    one = jnp.float32(1.0)
    got = []
    members = [totals]
    for m in range(1, GROUP):
        members.append(lax.ppermute(totals, "circ", [(i, i ^ m) for i in range(circ_count)]))
    got += members[1:]
    place = circ_place % GROUP
    sums = []
    for v in range(4):
        total = None
        for m in range(GROUP):
            weights = [steps[v // 2] ** ((p ^ m) if v % 2 else GROUP - 1 - (p ^ m)) for p in range(GROUP)]
            weight = jnp.float32(weights[0])
            for p in range(1, GROUP):
                weight = jnp.where(place == p, jnp.float32(weights[p]), weight)
            term = weight * members[m][v]
            total = term if total is None else total + term
        sums.append(total)
    totals = jnp.stack(sums)
    masks = {2: 4, 3: 8, 4: 16, 5: 48}
    for k in range(GROUP.bit_length() - 1, rounds):
        other = lax.ppermute(totals, "circ", [(i, i ^ masks[k]) for i in range(circ_count)])
        if k == rounds - 1:
            got += [totals, other]
            break
        got.append(other)
        on_right = ((circ_place >> k) & 1) == 1
        new = []
        for v in range(4):
            g = jnp.float32(merge[k, v // 2])
            grows = on_right if v % 2 else jnp.logical_not(on_right)
            own = jnp.where(grows, g, one)
            their = jnp.where(grows, one, g)
            new.append(own * totals[v] + their * other[v])
        totals = jnp.stack(new)
    coef = lax.dynamic_index_in_dim(jnp.asarray(table, f32), circ_place, 0, False)

    u_near = in_vmem(u)
    first, last = pl.pallas_call(
        edges_kernel,
        out_shape=(pltpu.VMEM((lines, REACH, width), f32),) * 2,
        in_specs=vmem(1),
        out_specs=tuple(vmem(2)),
        name="edges",
    )(u_near)
    ring = [(i, (i + 1) % circ_count) for i in range(circ_count)]
    gnir = [(j, i) for i, j in ring]
    left = lax.ppermute(last, "circ", ring)
    right = lax.ppermute(first, "circ", gnir)

    local, halo = circ_tables(cells)
    smem = [pl.BlockSpec(memory_space=pltpu.SMEM)]
    carries = [in_vmem(x) for x in got[:-1]]
    d_near, f_near, tile = pl.pallas_call(
        functools.partial(near_kernel, local, halo, len(carries), roots),
        out_shape=(pltpu.VMEM(u.shape, f32),) * 2 + (pltpu.VMEM((4, 8, width), f32),),
        in_specs=smem + vmem(3 + len(carries)),
        out_specs=tuple(vmem(3)),
        scratch_shapes=[pltpu.VMEM((4, lines, width), f32)],
        name="near",
    )(coef, u_near, in_vmem(right), in_vmem(left), *carries)

    ax_local, ax_gather, ax_spread = axial_tables(width, ax_count)
    rows = u.reshape(lines * cells, width)
    mine = lax.dynamic_index_in_dim(jnp.asarray(ax_gather, f32), ax_place, 0, False)
    sent = lax.dot_general(mine, rows, (((1,), (1,)), ((), ())), precision=PRECISE)
    near_side = lax.ppermute(sent, "ax", [(i, i ^ 1) for i in range(ax_count)])
    pair = jnp.concatenate([sent, near_side], axis=0)
    far_side = lax.ppermute(pair, "ax", [(i, i ^ 2) for i in range(ax_count)])
    square = lax.dynamic_index_in_dim(jnp.asarray(ax_local.swapaxes(1, 2), f32), ax_place, 0, False)
    ax_out = jnp.dot(rows, square, precision=PRECISE)
    order = np.asarray([[p ^ 1, p ^ 2, p ^ 3] for p in range(ax_count)])
    spread = np.stack([ax_spread[p][order[p]].reshape(12, width) for p in range(ax_count)])
    spread = lax.dynamic_index_in_dim(jnp.asarray(spread, f32), ax_place, 0, False)
    ax_in = jnp.concatenate([near_side, far_side], axis=0)
    ax_out = ax_out + lax.dot_general(ax_in, spread, (((0,), (0,)), ((), ())), precision=PRECISE)

    d_circ, filtered = pl.pallas_call(
        functools.partial(far_kernel, roots),
        out_shape=(jax.ShapeDtypeStruct(u.shape, f32),) * 2,
        in_specs=vmem(4),
        out_specs=(pl.BlockSpec(memory_space=pl.ANY),) * 2,
        scratch_shapes=[
            pltpu.VMEM((4, lines, width), f32),
            pltpu.VMEM((2, *u.shape), f32),
            pltpu.SemaphoreType.DMA((2, CHUNKS)),
        ],
        name="far",
    )(in_vmem(tile), in_vmem(got[-1]), in_vmem(d_near), in_vmem(f_near))
    shape = fields.shape
    return d_circ.reshape(shape), ax_out.reshape(shape), filtered.reshape(shape)


def solution(mesh):
    spec = P(None, None, "circ", "ax")

    return jax.shard_map(
        shards, mesh=mesh, in_specs=(spec,), out_specs=(spec, spec, spec), check_vma=False
    )
```

```python
import functools
import math

import jax
import jax.numpy as jnp
import numpy as np
from jax import lax
from jax.experimental import pallas as pl
from jax.experimental.pallas import tpu as pltpu
from jax.sharding import PartitionSpec as P


DERIV_NEAR = 14.0 / 9.0
DERIV_FAR = 1.0 / 9.0
ALPHA_DERIV = 1.0 / 3.0
ALPHA_FILTER = 0.4999
PRECISE = lax.Precision.HIGHEST
REACH = 4
CHUNKS = 4
GROUP = 4


def filter_terms(coupling):
    return [
        (193.0 + 126.0 * coupling) / 256.0,
        (105.0 + 302.0 * coupling) / 256.0,
        15.0 * (2.0 * coupling - 1.0) / 64.0,
        45.0 * (1.0 - 2.0 * coupling) / 512.0,
        5.0 * (2.0 * coupling - 1.0) / 256.0,
        (1.0 - 2.0 * coupling) / 512.0,
    ]


def root_of(coupling):
    return (-1.0 + math.sqrt(1.0 - 4.0 * coupling * coupling)) / (2.0 * coupling)


def stencils():
    deriv = {
        1: 0.5 * DERIV_NEAR,
        -1: -0.5 * DERIV_NEAR,
        2: 0.25 * DERIV_FAR,
        -2: -0.25 * DERIV_FAR,
    }
    terms = filter_terms(ALPHA_FILTER)
    smooth = {0: terms[0]}
    for offset in range(1, 6):
        smooth[offset] = smooth[-offset] = 0.5 * terms[offset]
    return [(ALPHA_DERIV, deriv), (ALPHA_FILTER, smooth)]


def line_kernel(coupling, stencil):
    root = root_of(coupling)
    gain = 1.0 / (1.0 + 2.0 * coupling * root)

    def h(n):
        return gain * math.fsum(c * root ** abs(n + m) for m, c in stencil.items())

    right = gain * math.fsum(c * root**m for m, c in stencil.items())
    left = gain * math.fsum(c * root ** (-m) for m, c in stencil.items())
    return root, h, right, left


def circ_tables(cells):
    local = np.zeros((2, cells, cells))
    halo = np.zeros((2, cells, cells))
    for which, (coupling, stencil) in enumerate(stencils()):
        root, h, right, left = line_kernel(coupling, stencil)
        for i in range(cells):
            for k in range(cells):
                local[which, i, k] = h(i - k)
            for m in range(cells):
                n = i - (cells + m) if m < REACH else i - (m - cells)
                if 0 < abs(n) <= REACH:
                    halo[which, i, m] = h(n) - (right if n > 0 else left) * root ** abs(n)
    return local, halo


def carry_tables(cells, count, group):
    first = group.bit_length() - 1
    rounds = count.bit_length() - 1
    later = rounds - first
    table = np.zeros((count, group - 1 + later + 1, 4))
    merge = np.zeros((rounds, 2))
    for which, (coupling, stencil) in enumerate(stencils()):
        root, _, right, left = line_kernel(coupling, stencil)
        step = root**cells
        wrap = 1.0 / (1.0 - step**count)
        for k in range(rounds):
            merge[k, which] = step ** (1 << k)
        for p in range(count):
            rows = table[p, :, 2 * which : 2 * which + 2]
            for m in range(1, group):
                q = p ^ m
                if q < p:
                    rows[m - 1, 0] = right * step ** (p - q - 1)
                else:
                    rows[m - 1, 1] = left * step ** (q - p - 1)
            for k in range(first, rounds):
                start = (p >> k) << k
                end = start + (1 << k) - 1
                last = k == rounds - 1
                slot = group - 1 + k - first + (1 if last else 0)
                factor = wrap if last else 1.0
                upper = (p >> k) & 1
                if upper or last:
                    rows[slot, 0] = right * factor * step ** (p - start if upper else p)
                if not upper or last:
                    rows[slot, 1] = left * factor * step ** (count - 1 - p if upper else end - p)
                if last:
                    rows[slot - 1, 0] = right * wrap * step ** (p + count - 1 - end)
                    rows[slot - 1, 1] = left * wrap * step ** (start + count - 1 - p)
    return table, merge


def bands_table(line_length):
    band_lower = np.full(line_length, ALPHA_DERIV)
    band_lower[0] = 0.0
    band_lower[1] = 0.25
    band_lower[line_length - 2] = 0.25
    band_lower[line_length - 1] = 2.0
    band_upper = np.full(line_length, ALPHA_DERIV)
    band_upper[0] = 2.0
    band_upper[1] = 0.25
    band_upper[line_length - 2] = 0.25
    band_upper[line_length - 1] = 0.0
    return band_lower, band_upper


def axial_stencil(line_length):
    s = np.zeros((line_length, line_length))
    for k in range(2, line_length - 2):
        s[k, k + 1] = 0.5 * DERIV_NEAR
        s[k, k - 1] = -0.5 * DERIV_NEAR
        s[k, k + 2] = 0.25 * DERIV_FAR
        s[k, k - 2] = -0.25 * DERIV_FAR
    s[0, :3] = (-2.5, 2.0, 0.5)
    s[1, 0], s[1, 2] = -0.75, 0.75
    e = line_length - 1
    s[e - 1, e - 2], s[e - 1, e] = -0.75, 0.75
    s[e, e - 2 : e + 1] = (-0.5, -2.0, 2.5)
    return s


def axial_tables(line_cells, count):
    n = line_cells * count
    low, up = bands_table(n)
    s = axial_stencil(n)
    t = np.eye(n) + np.diag(low[1:], -1) + np.diag(up[:-1], 1)
    inverse = np.linalg.inv(t)
    full = inverse @ s
    from_top = np.zeros(n)
    from_top[0] = 1.0
    for i in range(1, n):
        from_top[i] = 1.0 - low[i] * up[i - 1] / from_top[i - 1]
    from_end = np.zeros(n)
    from_end[n - 1] = 1.0
    for i in range(n - 2, -1, -1):
        from_end[i] = 1.0 - up[i] * low[i + 1] / from_end[i + 1]
    down = -low / from_end
    back = -up / from_top
    local = np.zeros((count, line_cells, line_cells))
    gather = np.zeros((count, 4, line_cells))
    grow_down = np.zeros((count, line_cells))
    grow_back = np.zeros((count, line_cells))
    corner = np.zeros((count, 2))
    for p in range(count):
        b, e = p * line_cells, (p + 1) * line_cells
        local[p] = full[b:e, b:e]
        grow_down[p] = np.cumprod(down[b:e])
        grow_back[p] = np.cumprod(back[b:e][::-1])[::-1]
        gather[p, 2, 0] = 1.0
        gather[p, 3, line_cells - 1] = 1.0
        if e < n:
            y = inverse[e - 1].copy()
            y[e:] = 0.0
            for k in range(e, e + 2):
                y[k] = inverse[k, k] / np.prod(down[e : k + 1])
            gather[p, 0] = (y @ s)[b:e]
        if b > 0:
            y = inverse[b].copy()
            y[:b] = 0.0
            for k in range(b - 2, b):
                y[k] = inverse[k, k] / np.prod(back[k:b])
            gather[p, 1] = (y @ s)[b:e]
    for p in range(count):
        b, e = p * line_cells, (p + 1) * line_cells
        if p > 0:
            corner[p, 0] = full[b, b - 1] - grow_down[p, 0] * gather[p - 1, 0, -1]
        if p < count - 1:
            corner[p, 1] = full[e - 1, e] - grow_back[p, -1] * gather[p + 1, 1, 0]
    spread = np.zeros((count, count, 4, line_cells))
    for p in range(count):
        weight = 1.0
        for q in range(p - 1, -1, -1):
            spread[p, q, 0] = weight * grow_down[p]
            weight *= grow_down[q, -1]
        weight = 1.0
        for q in range(p + 1, count):
            spread[p, q, 1] = weight * grow_back[p]
            weight *= grow_back[q, 0]
        if p > 0:
            spread[p, p - 1, 3, 0] = corner[p, 0]
        if p < count - 1:
            spread[p, p + 1, 2, -1] = corner[p, 1]
    return local, gather, spread


def by_row(values, shape):
    rows = lax.broadcasted_iota(jnp.int32, shape, len(shape) - 2)
    out = jnp.full(shape, float(values[0]), jnp.float32)
    for i in range(1, len(values)):
        out = jnp.where(rows == i, jnp.float32(values[i]), out)
    return out


def totals_kernel(weights, u_hbm, s_ref, u_ref, sems):
    lines, cells, width = u_ref.shape
    chunk = lines // CHUNKS
    copies = []
    for c in range(CHUNKS):
        part = pl.ds(c * chunk, chunk)
        copies.append(pltpu.make_async_copy(u_hbm.at[part], u_ref.at[part], sems.at[c]))
        copies[-1].start()
    w = [by_row(weights[v], (cells, width)) for v in range(4)]
    for c in range(CHUNKS):
        copies[c].wait()
        for n in range(c * chunk, (c + 1) * chunk):
            un = u_ref[n]
            for v in range(4):
                s_ref[v, n : n + 1, :] = jnp.sum(un * w[v], axis=0, keepdims=True)


def edges_kernel(u_ref, first_ref, last_ref):
    lines, cells, _ = u_ref.shape
    for n in range(lines):
        un = u_ref[n]
        first_ref[n] = un[:REACH]
        last_ref[n] = un[cells - REACH :]


def near_kernel(local, halo, count, roots, tile_ref, u_ref, right_ref, left_ref, *refs):
    got = refs[:count]
    d_ref, f_ref, lr = refs[count:]
    lines, cells, width = u_ref.shape
    outs = (d_ref, f_ref)
    for v in range(4):
        for n in range(0, lines, 8):
            part = slice(n, n + 8)
            total = got[0][v, part] * tile_ref[v]
            for k in range(1, count):
                total = total + got[k][v, part] * tile_ref[4 * k + v]
            lr[v, part] = total
    diag = {}
    for name, table in (("local", local), ("halo", halo)):
        for which in range(2):
            for s in range(cells):
                values = [table[which, i, (i - s) % cells] for i in range(cells)]
                if np.any(np.asarray(values) != 0.0):
                    diag[name, which, s] = by_row(values, (cells, width))
    ramps = ramp_rows(roots, cells, width)
    for n in range(lines):
        un = u_ref[n]
        hn = jnp.concatenate([right_ref[n], left_ref[n]], axis=0)
        acc = [
            ramps[2 * w] * jnp.broadcast_to(lr[2 * w, n : n + 1, :], (cells, width))
            + ramps[2 * w + 1] * jnp.broadcast_to(lr[2 * w + 1, n : n + 1, :], (cells, width))
            for w in range(2)
        ]
        for name, value in (("local", un), ("halo", hn)):
            for s in range(cells):
                used = [w for w in range(2) if (name, w, s) in diag]
                if not used:
                    continue
                turned = pltpu.roll(value, s, 0) if s else value
                for w in used:
                    acc[w] = acc[w] + turned * diag[name, w, s]
        for w in range(2):
            outs[w][n] = acc[w]


def ramp_rows(roots, cells, width):
    out = []
    for root in roots:
        out.append(by_row([root ** (i + 1) for i in range(cells)], (cells, width)))
        out.append(by_row([root ** (cells - i) for i in range(cells)], (cells, width)))
    return out


def far_kernel(roots, tile_ref, got, d_near, f_near, d_hbm, f_hbm, lr, done, sems):
    lines, cells, width = d_near.shape
    chunk = lines // CHUNKS
    ramps = ramp_rows(roots, cells, width)
    near = (d_near, f_near)
    hbm = (d_hbm, f_hbm)
    for v in range(4):
        for n in range(0, lines, 8):
            lr[v, n : n + 8] = got[v, n : n + 8] * tile_ref[tile_ref.shape[0] - 4 + v]
    copies = []
    for c in range(CHUNKS):
        part = pl.ds(c * chunk, chunk)
        for w in range(2):
            for n in range(c * chunk, (c + 1) * chunk):
                from_left = jnp.broadcast_to(lr[2 * w, n : n + 1, :], (cells, width))
                from_right = jnp.broadcast_to(lr[2 * w + 1, n : n + 1, :], (cells, width))
                done[w, n] = (
                    near[w][n] + ramps[2 * w] * from_left + ramps[2 * w + 1] * from_right
                )
            copies.append(
                pltpu.make_async_copy(done.at[w, part], hbm[w].at[part], sems.at[w, c])
            )
            copies[-1].start()
    for copy in copies:
        copy.wait()


def in_vmem(x):
    return pltpu.with_memory_space_constraint(x, pltpu.VMEM)


def vmem(count):
    return [pl.BlockSpec(memory_space=pltpu.VMEM)] * count


def shards(fields):
    parts, radial, cells, width = fields.shape
    lines = parts * radial
    u = fields.reshape(lines, cells, width)
    circ_count = lax.axis_size("circ")
    circ_place = lax.axis_index("circ")
    ax_count = lax.axis_size("ax")
    ax_place = lax.axis_index("ax")
    rounds = circ_count.bit_length() - 1
    roots = [root_of(ALPHA_DERIV), root_of(ALPHA_FILTER)]
    f32 = jnp.float32

    weights = np.zeros((4, cells))
    for which, root in enumerate(roots):
        weights[2 * which] = root ** (cells - 1.0 - np.arange(cells))
        weights[2 * which + 1] = root ** (1.0 * np.arange(cells))
    totals, u = pl.pallas_call(
        functools.partial(totals_kernel, weights),
        out_shape=(pltpu.VMEM((4, lines, width), f32), pltpu.VMEM(u.shape, f32)),
        in_specs=[pl.BlockSpec(memory_space=pl.ANY)],
        out_specs=tuple(vmem(2)),
        scratch_shapes=[pltpu.SemaphoreType.DMA((CHUNKS,))],
        name="totals",
    )(u)

    table, merge = carry_tables(cells, circ_count, GROUP)
    steps = [root**cells for root in roots]
    one = jnp.float32(1.0)
    got = []
    members = [totals]
    for m in range(1, GROUP):
        members.append(lax.ppermute(totals, "circ", [(i, i ^ m) for i in range(circ_count)]))
    got += members[1:]
    place = circ_place % GROUP
    sums = []
    for v in range(4):
        total = None
        for m in range(GROUP):
            weights = [steps[v // 2] ** ((p ^ m) if v % 2 else GROUP - 1 - (p ^ m)) for p in range(GROUP)]
            weight = jnp.float32(weights[0])
            for p in range(1, GROUP):
                weight = jnp.where(place == p, jnp.float32(weights[p]), weight)
            term = weight * members[m][v]
            total = term if total is None else total + term
        sums.append(total)
    totals = jnp.stack(sums)
    masks = {2: 4, 3: 8, 4: 16, 5: 48}
    for k in range(GROUP.bit_length() - 1, rounds):
        other = lax.ppermute(totals, "circ", [(i, i ^ masks[k]) for i in range(circ_count)])
        if k == rounds - 1:
            got += [totals, other]
            break
        got.append(other)
        on_right = ((circ_place >> k) & 1) == 1
        new = []
        for v in range(4):
            g = jnp.float32(merge[k, v // 2])
            grows = on_right if v % 2 else jnp.logical_not(on_right)
            own = jnp.where(grows, g, one)
            their = jnp.where(grows, one, g)
            new.append(own * totals[v] + their * other[v])
        totals = jnp.stack(new)
    coef = lax.dynamic_index_in_dim(jnp.asarray(table, f32), circ_place, 0, False)

    u_near = in_vmem(u)
    first, last = pl.pallas_call(
        edges_kernel,
        out_shape=(pltpu.VMEM((lines, REACH, width), f32),) * 2,
        in_specs=vmem(1),
        out_specs=tuple(vmem(2)),
        name="edges",
    )(u_near)
    ring = [(i, (i + 1) % circ_count) for i in range(circ_count)]
    gnir = [(j, i) for i, j in ring]
    left = lax.ppermute(last, "circ", ring)
    right = lax.ppermute(first, "circ", gnir)

    local, halo = circ_tables(cells)
    tile = jnp.broadcast_to(coef.reshape(-1, 1, 1), (coef.size, 8, width))
    tile = in_vmem(lax.optimization_barrier(tile))
    carries = [in_vmem(x) for x in got[:-1]]
    d_near, f_near = pl.pallas_call(
        functools.partial(near_kernel, local, halo, len(carries), roots),
        out_shape=(pltpu.VMEM(u.shape, f32),) * 2,
        in_specs=vmem(4 + len(carries)),
        out_specs=tuple(vmem(2)),
        scratch_shapes=[pltpu.VMEM((4, lines, width), f32)],
        name="near",
    )(tile, u_near, in_vmem(right), in_vmem(left), *carries)

    ax_local, ax_gather, ax_spread = axial_tables(width, ax_count)
    rows = u.reshape(lines * cells, width)
    mine = lax.dynamic_index_in_dim(jnp.asarray(ax_gather, f32), ax_place, 0, False)
    sent = lax.dot_general(mine, rows, (((1,), (1,)), ((), ())), precision=PRECISE)
    near_side = lax.ppermute(sent, "ax", [(i, i ^ 1) for i in range(ax_count)])
    pair = jnp.concatenate([sent, near_side], axis=0)
    far_side = lax.ppermute(pair, "ax", [(i, i ^ 2) for i in range(ax_count)])
    square = lax.dynamic_index_in_dim(jnp.asarray(ax_local.swapaxes(1, 2), f32), ax_place, 0, False)
    ax_out = jnp.dot(rows, square, precision=PRECISE)
    order = np.asarray([[p ^ 1, p ^ 2, p ^ 3] for p in range(ax_count)])
    spread = np.stack([ax_spread[p][order[p]].reshape(12, width) for p in range(ax_count)])
    spread = lax.dynamic_index_in_dim(jnp.asarray(spread, f32), ax_place, 0, False)
    spread = lax.optimization_barrier(spread)
    ax_in = jnp.concatenate([near_side, far_side], axis=0)
    ax_out = ax_out + lax.dot_general(ax_in, spread, (((0,), (0,)), ((), ())), precision=PRECISE)

    d_circ, filtered = pl.pallas_call(
        functools.partial(far_kernel, roots),
        out_shape=(jax.ShapeDtypeStruct(u.shape, f32),) * 2,
        in_specs=vmem(4),
        out_specs=(pl.BlockSpec(memory_space=pl.ANY),) * 2,
        scratch_shapes=[
            pltpu.VMEM((4, lines, width), f32),
            pltpu.VMEM((2, *u.shape), f32),
            pltpu.SemaphoreType.DMA((2, CHUNKS)),
        ],
        name="far",
    )(tile, in_vmem(got[-1]), in_vmem(d_near), in_vmem(f_near))
    shape = fields.shape
    return d_circ.reshape(shape), ax_out.reshape(shape), filtered.reshape(shape)


def solution(mesh):
    spec = P(None, None, "circ", "ax")

    return jax.shard_map(
        shards, mesh=mesh, in_specs=(spec,), out_specs=(spec, spec, spec), check_vma=False
    )
```
